32 devices in a mesh: wide: 16 (over z, y, core), narrow: 2 (over x).
Axes of the slice: x: 2, y: 2, z: 4, core: 2. Of those that a mesh axis runs over, the one named last changes fastest.
Arguments:
- valence: float32 [8, 32768], P(None, ('wide', 'narrow')), may hold values from -6 to 6
- conduction: float32 [32, 32768], P(('wide', 'narrow')), may hold values from -6 to 6
- eps_val: float32 [8], replicated, may hold values from -12 to -2
- eps_cond: float32 [32], replicated, may hold values from 0.5 to 20
- omega: float32 [6], replicated, may hold values from 0.3 to 30
- gmap: int32 [8192], replicated, may hold values from 0 to 32767, as said below
Outputs:
- chi: float32 [6, 8192, 8192], P(None, 'wide', 'narrow')
The draws below stay inside these ranges and needn't reach their ends.
Inputs may be any that keep to these rules, and one draw needn't show every extreme that they name: `gmap`: distinct grid indices: the 8192 grid points of smallest squared wave vector (frequencies folded to -16 .. 15), equal lengths in random order, listed by rising length.
All inputs are finite; a program needn't handle non-finite values.
Results may differ from the reference program's by a relative error of at most 0.0042.
Values may be sent and summed in bfloat16 or wider, within the bound.
A program may use at most 128 MiB of HBM per device.

```python
import math
import jax
import jax.numpy as jnp
from jax import lax

GRID = 32
NPW = 8192
NV = 8
NW = 6
NGRID = 32768
NC = 32
NPAIR = 256


def draw_gmap(key, part):
    flat_index = jnp.arange(GRID * GRID * GRID, dtype=jnp.int32)
    coord_x = flat_index // (GRID * GRID)
    coord_y = flat_index // GRID % GRID
    coord_z = flat_index % GRID
    fold_x = jnp.where(coord_x < GRID // 2, coord_x, coord_x - GRID)
    fold_y = jnp.where(coord_y < GRID // 2, coord_y, coord_y - GRID)
    fold_z = jnp.where(coord_z < GRID // 2, coord_z, coord_z - GRID)
    length_sq = fold_x * fold_x + fold_y * fold_y + fold_z * fold_z
    tiebreak = jax.random.permutation(jax.random.fold_in(key, 17), GRID * GRID * GRID).astype(jnp.int32)
    scores = length_sq * (GRID * GRID * GRID) + tiebreak
    ordered = jnp.argsort(scores, stable=True)
    return ordered[:NPW].astype(jnp.int32)


def block_scale(stream_key, dims, split, low, high):
    level, own = 1.0, jax.random.fold_in(stream_key, 6)
    for position, parts in split:
        draws = jnp.exp(jax.random.uniform(jax.random.fold_in(own, position), (parts,), jnp.float32, low / len(split), high / len(split)))
        level = level * jnp.repeat(draws, dims[position] // parts).reshape([-1 if axis == position else 1 for axis in range(len(dims))])
    return level


def centred(stream_key, shape, width, limit, cuts=(), kind=jnp.bfloat16):
    result = jax.random.normal(stream_key, shape, jnp.float32) * width
    if len(cuts) > 0:
        result = block_scale(stream_key, shape, cuts, -0.22, 0.18) * result
    return jnp.clip(result, min=-limit, max=limit).astype(kind)


def setup_inputs(seed: int = 0) -> dict:
    key_of = jax.random.split(jax.random.key(seed), 7)
    valence = centred(key_of[0], (NV, NGRID), 1.0, 6.0, ((1, 32),), jnp.float32)
    conduction = centred(key_of[1], (NC, NGRID), 1.0, 6.0, ((0, 32),), jnp.float32)
    eps_val = jnp.clip(jax.random.uniform(key_of[2], (NV,), jnp.float32, -12.0, -2.0), -12.0, -2.0)
    eps_cond = jnp.clip(jax.random.uniform(key_of[3], (NC,), jnp.float32, 0.5, 20.0), 0.5, 20.0)
    omega = jnp.clip(jnp.exp(jax.random.uniform(key_of[4], (NW,), jnp.float32, math.log(0.3), math.log(30.0))), 0.3, 30.0)
    gmap = draw_gmap(jax.random.fold_in(key_of[6], 71), 0)
    return dict(valence=valence, conduction=conduction, eps_val=eps_val, eps_cond=eps_cond, omega=omega, gmap=gmap)


def reference(valence, conduction, eps_val, eps_cond, omega, gmap):
    cube = valence.reshape(NV, GRID, GRID, GRID)
    norm_factor = 1.0 / jnp.sqrt(jnp.float32(NGRID))

    def one_band(band):
        product = cube * band.reshape(1, GRID, GRID, GRID)
        spectrum = jnp.fft.fftn(product, axes=(1, 2, 3)).reshape(NV, NGRID)
        picked = spectrum[:, gmap] * norm_factor
        return jnp.stack([jnp.real(picked), jnp.imag(picked)]).astype(jnp.bfloat16)
    stacked = lax.map(one_band, conduction)
    pairs = jnp.transpose(stacked, (1, 0, 2, 3)).reshape(2, NPAIR, NPW)
    energy_gap = (eps_cond[:, None] - eps_val[None, :]).reshape(NPAIR)
    weights = -2.0 * energy_gap[None, :] / (energy_gap[None, :] ** 2 + omega[:, None] ** 2)
    weights = weights / jnp.sqrt(jnp.float32(NPAIR))
    pair_float = pairs.astype(jnp.float32).reshape(2 * NPAIR, NPW)

    def one_freq(row_weight):
        scaled = (pairs.astype(jnp.float32) * row_weight[None, :, None]).astype(jnp.bfloat16)
        scaled = lax.optimization_barrier(scaled).astype(jnp.float32).reshape(2 * NPAIR, NPW)
        return jnp.dot(scaled.T, pair_float, preferred_element_type=jnp.float32, precision=lax.Precision.HIGHEST)
    return lax.map(one_freq, weights)
```

```python
import functools
import math

import jax
import jax.numpy as jnp
import numpy as np
from jax import lax
from jax.experimental import pallas as pl
from jax.experimental.pallas import tpu as pltpu
from jax.sharding import PartitionSpec as P

GRID = 32
MESH = pl.DeviceIdType.MESH
VMEM = pltpu.MemorySpace.VMEM


def wide_factors(wide):
    chips = wide // 2
    inner = 2 ** (int(math.log2(chips)) // 2)
    return chips // inner, inner


def gather_kernel(wide, narrow, split, row_width, src, out, *rest):
    if row_width:
        rows, send_sem, recv_sem, own_sem, row_send, row_recv = rest
    else:
        send_sem, recv_sem, own_sem = rest
    outer, inner = wide_factors(wide)
    w, n = lax.axis_index("wide"), lax.axis_index("narrow")
    core = lax.rem(w, 2)
    y = lax.rem(w // 2, inner)
    z = w // (2 * inner)

    def wide_at(zz, yy, cc):
        return (zz * inner + yy) * 2 + cc

    def slot(zz, yy, cc, nn):
        return wide_at(zz, yy, cc) * narrow + nn

    xs = [lax.rem(n + i, narrow) for i in range(1, narrow)]
    zs = [lax.rem(z + i, outer) for i in range(1, outer)]
    ys = [lax.rem(y + i, inner) for i in range(1, inner)]
    to_x = [(w, nn) for nn in xs]
    to_z = [(wide_at(zz, y, core), n) for zz in zs]
    to_y = [(wide_at(z, yy, core), n) for yy in ys]
    to_core = [(wide_at(z, y, 1 - core), n)]
    peers = to_x + to_z + to_y + to_core

    barrier = pltpu.get_barrier_semaphore()
    for peer in peers:
        pl.semaphore_signal(barrier, inc=1, device_id=peer, device_id_type=MESH)
    pl.semaphore_wait(barrier, len(peers))

    def piece(nn):
        if split:
            return src.at[:, pl.ds(pl.multiple_of(nn * split, split), split)]
        return src

    started = []

    def send(ref, index, target):
        copy = pltpu.make_async_remote_copy(
            src_ref=ref,
            dst_ref=out.at[index],
            send_sem=send_sem.at[len(started)],
            recv_sem=recv_sem.at[index],
            device_id=target,
            device_id_type=MESH,
        )
        copy.start()
        started.append(copy)

    def arrived(index):
        pltpu.make_async_remote_copy(
            src_ref=out.at[index],
            dst_ref=out.at[index],
            send_sem=send_sem.at[0],
            recv_sem=recv_sem.at[index],
            device_id=to_core[0],
            device_id_type=MESH,
        ).wait_recv()

    mine = slot(z, y, core, n)
    for target in to_x:
        send(piece(target[1]), mine, target)
    for target in to_z + to_y + to_core:
        send(piece(n), mine, target)
    own = pltpu.make_async_copy(piece(n), out.at[mine], own_sem)
    own.start()
    for nn in xs:
        index = slot(z, y, core, nn)
        arrived(index)
        for target in to_z + to_y + to_core:
            send(out.at[index], index, target)
    for zz in zs:
        for nn in [n] + xs:
            index = slot(zz, y, core, nn)
            arrived(index)
            for target in to_y + to_core:
                send(out.at[index], index, target)
    for yy in ys:
        for zz in [z] + zs:
            for nn in [n] + xs:
                index = slot(zz, yy, core, nn)
                arrived(index)
                send(out.at[index], index, to_core[0])
    own.wait()

    if row_width:
        holder = w // (wide // narrow)
        first = pl.multiple_of(lax.rem(w, wide // narrow) * row_width, 128)
        group = 2 * narrow

    def row_copy(index, target, start, sem):
        return pltpu.make_async_remote_copy(
            src_ref=out.at[pl.ds(start, group), :, pl.ds(first, row_width)],
            dst_ref=rows.at[pl.ds(start, group)],
            send_sem=row_send.at[sem],
            recv_sem=row_recv.at[index],
            device_id=target,
            device_id_type=MESH,
        )

    chips = [(zz, yy) for yy in [y] + ys for zz in [z] + zs]
    for number, (zz, yy) in enumerate(chips):
        for nn in [n] + xs:
            arrived(slot(zz, yy, 1 - core, nn))
        if row_width:
            @pl.when(n == holder)
            def _():
                for k, target in enumerate(to_x):
                    row_copy(number, target, slot(zz, yy, 0, 0), number * len(to_x) + k).start()

    for copy in started:
        copy.wait_send()
    if row_width:
        @pl.when(n == holder)
        def _():
            rows[...] = out[:, :, pl.ds(first, row_width)]
            for number, (zz, yy) in enumerate(chips):
                for k, target in enumerate(to_x):
                    row_copy(number, target, slot(zz, yy, 0, 0), number * len(to_x) + k).wait_send()

        @pl.when(n != holder)
        def _():
            for number, (zz, yy) in enumerate(chips):
                row_copy(number, to_x[0], slot(zz, yy, 0, 0), 0).wait_recv()


def gather(src, wide, narrow, split, row_width, collective_id):
    outer, inner = wide_factors(wide)
    devices = wide * narrow
    n_x, n_z, n_y = narrow - 1, outer - 1, inner - 1
    sends = n_x + n_z + n_y + 1
    sends += n_x * (n_z + n_y + 1) + n_z * narrow * (n_y + 1) + n_y * outer * narrow
    block = (src.shape[0], split or src.shape[1])
    out_shape = [jax.ShapeDtypeStruct((devices,) + block, src.dtype)]
    scratch = [
        pltpu.SemaphoreType.DMA((sends,)),
        pltpu.SemaphoreType.DMA((devices,)),
        pltpu.SemaphoreType.DMA,
    ]
    if row_width:
        out_shape.append(jax.ShapeDtypeStruct((devices, src.shape[0], row_width), src.dtype))
        scratch.append(pltpu.SemaphoreType.DMA((outer * inner * n_x,)))
        scratch.append(pltpu.SemaphoreType.DMA((outer * inner,)))
    return pl.pallas_call(
        functools.partial(gather_kernel, wide, narrow, split, row_width),
        out_shape=out_shape,
        in_specs=[pl.BlockSpec(memory_space=VMEM)],
        out_specs=[pl.BlockSpec(memory_space=VMEM)] * len(out_shape),
        scratch_shapes=scratch,
        compiler_params=pltpu.CompilerParams(
            collective_id=collective_id, has_side_effects=True, vmem_limit_bytes=48 << 20
        ),
    )(src)


@functools.lru_cache(None)
def tables(num_waves, num_val):
    fold = np.arange(GRID)
    fold = np.where(fold < GRID // 2, fold, fold - GRID)
    squares = fold**2
    lengths = (squares[:, None, None] + squares[None, :, None] + squares[None, None, :]).reshape(-1)
    limit = int(np.sort(lengths)[num_waves - 1])
    reach = math.isqrt(limit)
    assert reach < GRID // 2
    half = [
        (ky, kz)
        for ky in range(-reach, reach + 1)
        for kz in range(0, reach + 1)
        if ky * ky + kz * kz <= limit and (kz > 0 or ky >= 0)
    ]
    count = -(-len(half) // 128) * 128
    kys = np.array([k for k, _ in half])
    kzs = np.array([k for _, k in half])
    points = np.arange(GRID)
    turn = 2.0 * np.pi / GRID
    phase = (points[:, None, None] * kys + points[None, :, None] * kzs) % GRID
    phase = phase.reshape(GRID * GRID, len(half)) * turn
    plane = np.zeros((GRID * GRID, 2 * count))
    plane[:, : len(half)] = np.cos(phase)
    plane[:, count : count + len(half)] = -np.sin(phase)
    codes = np.full((count, 2), -1, np.int32)
    codes[: len(half), 0] = (kys % GRID) * GRID + kzs % GRID
    codes[: len(half), 1] = (-kys % GRID) * GRID + -kzs % GRID
    kxs = np.arange(-reach, reach + 1)
    line = (kxs[:, None] * points[None, :] % GRID) * turn
    eye = np.eye(num_val)
    norm = 1.0 / math.sqrt(GRID**3)
    cosine = np.kron(np.cos(line), eye) * norm
    sine = np.kron(np.sin(line), eye) * norm
    return plane, codes, np.stack([cosine, sine]), reach


def np_halves(table):
    table = np.asarray(table, np.float32)
    high = table.astype(jnp.bfloat16)
    return high, (table - high.astype(np.float32)).astype(jnp.bfloat16)


def split_bf16(x):
    high = x.astype(jnp.bfloat16)
    return high, (x - high.astype(jnp.float32)).astype(jnp.bfloat16)


def dot(a, b):
    return jnp.dot(a, b, preferred_element_type=jnp.float32)


def dot3(a, b_high, b_low):
    a_high, a_low = split_bf16(a)
    return dot(a_high, b_high) + (dot(a_low, b_high) + dot(a_high, b_low))


def dot3_left(a_high, a_low, b):
    b_high, b_low = split_bf16(b)
    return dot(a_high, b_high) + (dot(a_high, b_low) + dot(a_low, b_high))


def pair_kernel(reach, tile, val, cond, gmap, plane_h, plane_l, codes, line_h, line_l, out, field, picked):
    xs, num_val, plane = val.shape
    count = codes.shape[0]
    kinds = 2 * reach + 1
    field[...] = (val[...] * cond[...]).reshape(xs * num_val, plane)
    step = dot3(field[...], plane_h[...], plane_l[...])
    real, imag = step[:, :count], step[:, count:]
    size = kinds * num_val
    cos_h, sin_h, cos_l, sin_l = line_h[0], line_h[1], line_l[0], line_l[1]
    picked[:size, :] = dot3_left(cos_h, cos_l, real) + dot3_left(sin_h, sin_l, imag)
    picked[size:, :] = dot3_left(cos_h, cos_l, imag) - dot3_left(sin_h, sin_l, real)
    source = picked[...].astype(jnp.bfloat16)
    first, second = codes[:, 0:1], codes[:, 1:2]

    def body(t, carry):
        here = pl.ds(pl.multiple_of(t * tile, tile), tile)
        index = gmap[:, here]
        kx = index // (GRID * GRID)
        code = index % (GRID * GRID)
        ky, kz = code // GRID, code % GRID
        kx = jnp.where(kx < GRID // 2, kx, kx - GRID)
        direct = ((kz > 0) & (kz < GRID // 2)) | ((kz == 0) & (ky < GRID // 2))
        kx = jnp.where(direct, kx, -kx) + reach
        sign = jnp.where(direct, 1.0, -1.0).astype(jnp.float32)
        hit = (code == first) | (code == second)
        columns = dot(source, jnp.where(hit, 1.0, 0.0).astype(jnp.bfloat16))
        columns = columns.reshape(2, kinds, num_val, tile)
        real = jnp.zeros((num_val, tile), jnp.float32)
        imag = jnp.zeros((num_val, tile), jnp.float32)
        for k in range(kinds):
            keep = jnp.broadcast_to(kx == k, (num_val, tile))
            real = jnp.where(keep, columns[0, k], real)
            imag = jnp.where(keep, columns[1, k], imag)
        out[:, here] = jnp.concatenate([real, imag * sign], axis=0).astype(jnp.bfloat16)
        return carry

    lax.fori_loop(0, out.shape[1] // tile, body, 0)


def transform_pairs(val, cond, gmap):
    xs, num_val, plane = val.shape
    waves = gmap.shape[1]
    table, codes, line, reach = tables(waves, num_val)
    plane_h, plane_l = np_halves(table)
    line_h, line_l = np_halves(line)
    count = codes.shape[0]
    return pl.pallas_call(
        functools.partial(pair_kernel, reach, min(512, waves)),
        out_shape=jax.ShapeDtypeStruct((2 * num_val, waves), jnp.bfloat16),
        in_specs=[pl.BlockSpec(memory_space=VMEM)] * 8,
        out_specs=pl.BlockSpec(memory_space=VMEM),
        scratch_shapes=[
            pltpu.VMEM((xs * num_val, plane), jnp.float32),
            pltpu.VMEM((2 * (2 * reach + 1) * num_val, count), jnp.float32),
        ],
        compiler_params=pltpu.CompilerParams(vmem_limit_bytes=48 << 20),
    )(val, cond, gmap, jnp.asarray(plane_h), jnp.asarray(plane_l), jnp.asarray(codes), jnp.asarray(line_h), jnp.asarray(line_l))


def chi_kernel(weights, rows, columns, out, scaled):
    @pl.when(pl.program_id(1) == 0)
    def _():
        scale = rows[...].astype(jnp.float32) * weights[0]
        scaled[...] = scale.T.astype(jnp.bfloat16)

    out[0] = dot(scaled[...], columns[...])


def chi_of(weights, rows, columns):
    depth, row_width = rows.shape
    width = columns.shape[1]
    num = weights.shape[0]
    tile = min(1024, width)
    return pl.pallas_call(
        chi_kernel,
        grid=(num, width // tile),
        out_shape=jax.ShapeDtypeStruct((num, row_width, width), jnp.float32),
        in_specs=[
            pl.BlockSpec((1, depth, 1), lambda w, c: (w, 0, 0)),
            pl.BlockSpec((depth, row_width), lambda w, c: (0, 0)),
            pl.BlockSpec((depth, tile), lambda w, c: (0, c)),
        ],
        out_specs=pl.BlockSpec((1, row_width, tile), lambda w, c: (w, 0, c)),
        scratch_shapes=[pltpu.VMEM((row_width, depth), jnp.bfloat16)],
        compiler_params=pltpu.CompilerParams(vmem_limit_bytes=48 << 20),
    )(weights, rows, columns)


def body(valence, conduction, eps_val, eps_cond, omega, gmap):
    wide, narrow = lax.axis_size("wide"), lax.axis_size("narrow")
    devices = wide * narrow
    num_val, chunk = valence.shape
    num_local = conduction.shape[0]
    assert num_local == 1
    plane = GRID * GRID
    waves = gmap.shape[0]
    [full] = gather(valence, wide, narrow, 0, 0, 0)
    if chunk != plane:
        full = full.reshape(GRID, devices // GRID, num_val, chunk)
        full = jnp.transpose(full, (0, 2, 1, 3)).reshape(GRID, num_val, plane)
    local = transform_pairs(full, conduction.reshape(GRID, 1, plane), gmap.reshape(1, waves))
    columns, rows = gather(local, wide, narrow, waves // narrow, waves // wide, 1)
    depth = devices * 2 * num_val
    columns = columns.reshape(depth, waves // narrow)
    rows = rows.reshape(depth, waves // wide)
    num_pairs = num_val * eps_cond.shape[0]
    gap = eps_cond[:, None] - eps_val[None, :]
    gap = jnp.stack([gap, gap], axis=1).reshape(depth)
    weights = -2.0 * gap[None, :] / (gap[None, :] ** 2 + omega[:, None] ** 2)
    weights = weights / jnp.sqrt(jnp.float32(num_pairs))
    return chi_of(weights[:, :, None], rows, columns)


def solution(mesh):
    placed = (P(None, ("wide", "narrow")), P(("wide", "narrow"), None), P(), P(), P(), P())
    return jax.shard_map(
        body, mesh=mesh, in_specs=placed, out_specs=P(None, "wide", "narrow"), check_vma=False
    )
```

```python
import functools
import math

import jax
import jax.numpy as jnp
import numpy as np
from jax import lax
from jax.experimental import pallas as pl
from jax.experimental.pallas import tpu as pltpu
from jax.sharding import PartitionSpec as P

GRID = 32
MESH = pl.DeviceIdType.MESH
VMEM = pltpu.MemorySpace.VMEM
HBM = pltpu.MemorySpace.HBM
SMEM = pltpu.MemorySpace.SMEM


def wide_factors(wide):
    chips = wide // 2
    inner = 2 ** (int(math.log2(chips)) // 2)
    return chips // inner, inner


def gather_kernel(wide, narrow, split, row_width, src, out, *rest):
    if row_width:
        rows, send_sem, recv_sem, own_sem, row_send, row_recv = rest
    else:
        send_sem, recv_sem, own_sem = rest
    outer, inner = wide_factors(wide)
    w, n = lax.axis_index("wide"), lax.axis_index("narrow")
    core = lax.rem(w, 2)
    y = lax.rem(w // 2, inner)
    z = w // (2 * inner)

    def wide_at(zz, yy, cc):
        return (zz * inner + yy) * 2 + cc

    def slot(zz, yy, cc, nn):
        return wide_at(zz, yy, cc) * narrow + nn

    xs = [lax.rem(n + i, narrow) for i in range(1, narrow)]
    zs = [lax.rem(z + i, outer) for i in range(1, outer)]
    ys = [lax.rem(y + i, inner) for i in range(1, inner)]
    to_x = [(w, nn) for nn in xs]
    to_z = [(wide_at(zz, y, core), n) for zz in zs]
    to_y = [(wide_at(z, yy, core), n) for yy in ys]
    to_core = [(wide_at(z, y, 1 - core), n)]
    peers = to_x + to_z + to_y + to_core

    barrier = pltpu.get_barrier_semaphore()
    for peer in peers:
        pl.semaphore_signal(barrier, inc=1, device_id=peer, device_id_type=MESH)
    pl.semaphore_wait(barrier, len(peers))

    def piece(nn):
        if split:
            return src.at[:, pl.ds(pl.multiple_of(nn * split, split), split)]
        return src

    started = []

    def send(ref, index, target):
        copy = pltpu.make_async_remote_copy(
            src_ref=ref,
            dst_ref=out.at[index],
            send_sem=send_sem.at[len(started)],
            recv_sem=recv_sem.at[index],
            device_id=target,
            device_id_type=MESH,
        )
        copy.start()
        started.append(copy)

    def arrived(index):
        pltpu.make_async_remote_copy(
            src_ref=out.at[index],
            dst_ref=out.at[index],
            send_sem=send_sem.at[0],
            recv_sem=recv_sem.at[index],
            device_id=to_core[0],
            device_id_type=MESH,
        ).wait_recv()

    mine = slot(z, y, core, n)
    for target in to_x:
        send(piece(target[1]), mine, target)
    for target in to_z + to_y + to_core:
        send(piece(n), mine, target)
    own = pltpu.make_async_copy(piece(n), out.at[mine], own_sem)
    own.start()
    for nn in xs:
        index = slot(z, y, core, nn)
        arrived(index)
        for target in to_z + to_y + to_core:
            send(out.at[index], index, target)
    for zz in zs:
        for nn in [n] + xs:
            index = slot(zz, y, core, nn)
            arrived(index)
            for target in to_y + to_core:
                send(out.at[index], index, target)
    for yy in ys:
        for zz in [z] + zs:
            for nn in [n] + xs:
                index = slot(zz, yy, core, nn)
                arrived(index)
                send(out.at[index], index, to_core[0])
    own.wait()

    if row_width:
        holder = w // (wide // narrow)
        first = pl.multiple_of(lax.rem(w, wide // narrow) * row_width, 128)
        group = 2 * narrow

    def row_copy(index, target, start, sem):
        return pltpu.make_async_remote_copy(
            src_ref=out.at[pl.ds(start, group), :, pl.ds(first, row_width)],
            dst_ref=rows.at[pl.ds(start, group)],
            send_sem=row_send.at[sem],
            recv_sem=row_recv.at[index],
            device_id=target,
            device_id_type=MESH,
        )

    chips = [(zz, yy) for yy in [y] + ys for zz in [z] + zs]
    for number, (zz, yy) in enumerate(chips):
        for nn in [n] + xs:
            arrived(slot(zz, yy, 1 - core, nn))
        if row_width:
            @pl.when(n == holder)
            def _():
                for k, target in enumerate(to_x):
                    row_copy(number, target, slot(zz, yy, 0, 0), number * len(to_x) + k).start()

    for copy in started:
        copy.wait_send()
    if row_width:
        @pl.when(n == holder)
        def _():
            rows[...] = out[:, :, pl.ds(first, row_width)]
            for number, (zz, yy) in enumerate(chips):
                for k, target in enumerate(to_x):
                    row_copy(number, target, slot(zz, yy, 0, 0), number * len(to_x) + k).wait_send()

        @pl.when(n != holder)
        def _():
            for number, (zz, yy) in enumerate(chips):
                row_copy(number, to_x[0], slot(zz, yy, 0, 0), 0).wait_recv()


def gather(src, wide, narrow, split, row_width, collective_id):
    outer, inner = wide_factors(wide)
    devices = wide * narrow
    n_x, n_z, n_y = narrow - 1, outer - 1, inner - 1
    sends = n_x + n_z + n_y + 1
    sends += n_x * (n_z + n_y + 1) + n_z * narrow * (n_y + 1) + n_y * outer * narrow
    block = (src.shape[0], split or src.shape[1])
    out_shape = [jax.ShapeDtypeStruct((devices,) + block, src.dtype)]
    scratch = [
        pltpu.SemaphoreType.DMA((sends,)),
        pltpu.SemaphoreType.DMA((devices,)),
        pltpu.SemaphoreType.DMA,
    ]
    if row_width:
        out_shape.append(jax.ShapeDtypeStruct((devices, src.shape[0], row_width), src.dtype))
        scratch.append(pltpu.SemaphoreType.DMA((outer * inner * n_x,)))
        scratch.append(pltpu.SemaphoreType.DMA((outer * inner,)))
    return pl.pallas_call(
        functools.partial(gather_kernel, wide, narrow, split, row_width),
        out_shape=out_shape,
        in_specs=[pl.BlockSpec(memory_space=pl.ANY)],
        out_specs=[pl.BlockSpec(memory_space=VMEM if row_width else pl.ANY)] * len(out_shape),
        scratch_shapes=scratch,
        compiler_params=pltpu.CompilerParams(
            collective_id=collective_id, has_side_effects=True, vmem_limit_bytes=(48 if row_width else 63) << 20
        ),
    )(src)


@functools.lru_cache(None)
def tables(num_waves, num_val):
    fold = np.arange(GRID)
    fold = np.where(fold < GRID // 2, fold, fold - GRID)
    squares = fold**2
    lengths = (squares[:, None, None] + squares[None, :, None] + squares[None, None, :]).reshape(-1)
    limit = int(np.sort(lengths)[num_waves - 1])
    reach = math.isqrt(limit)
    assert reach < GRID // 2
    half = [
        (ky, kz)
        for ky in range(-reach, reach + 1)
        for kz in range(0, reach + 1)
        if ky * ky + kz * kz <= limit and (kz > 0 or ky >= 0)
    ]
    count = -(-len(half) // 128) * 128
    kys = np.array([k for k, _ in half])
    kzs = np.array([k for _, k in half])
    points = np.arange(GRID)
    turn = 2.0 * np.pi / GRID
    phase = (points[:, None, None] * kys + points[None, :, None] * kzs) % GRID
    phase = phase.reshape(GRID * GRID, len(half)) * turn
    plane = np.zeros((GRID * GRID, 2 * count))
    plane[:, : len(half)] = np.cos(phase)
    plane[:, count : count + len(half)] = -np.sin(phase)
    codes = np.full((count, 2), -1, np.int32)
    codes[: len(half), 0] = (kys % GRID) * GRID + kzs % GRID
    codes[: len(half), 1] = (-kys % GRID) * GRID + -kzs % GRID
    kxs = np.arange(-reach, reach + 1)
    line = (kxs[:, None] * points[None, :] % GRID) * turn
    eye = np.eye(num_val)
    norm = 1.0 / math.sqrt(GRID**3)
    cosine = np.kron(np.cos(line), eye) * norm
    sine = np.kron(np.sin(line), eye) * norm
    return plane, codes, np.stack([cosine, sine]), reach


def np_halves(table):
    table = np.asarray(table, np.float32)
    high = table.astype(jnp.bfloat16)
    return high, (table - high.astype(np.float32)).astype(jnp.bfloat16)


def split_bf16(x):
    high = x.astype(jnp.bfloat16)
    return high, (x - high.astype(jnp.float32)).astype(jnp.bfloat16)


def dot(a, b):
    return jnp.dot(a, b, preferred_element_type=jnp.float32)


def dot3(a, b_high, b_low):
    a_high, a_low = split_bf16(a)
    return dot(a_high, b_high) + (dot(a_low, b_high) + dot(a_high, b_low))


def dot3_left(a_high, a_low, b):
    b_high, b_low = split_bf16(b)
    return dot(a_high, b_high) + (dot(a_high, b_low) + dot(a_low, b_high))


def pair_kernel(reach, tile, *refs):
    sources, out, field, picked = refs[:8], refs[8], refs[9], refs[10]
    held, sems = refs[11:19], refs[19]
    copies = [pltpu.make_async_copy(a, b, sems.at[i]) for i, (a, b) in enumerate(zip(sources, held))]
    for copy in copies:
        copy.start()
    val, cond, plane_h, plane_l, line_h, line_l, codes, gmap = held
    for copy in copies:
        copy.wait()
    xs, num_val, plane = val.shape
    count = codes.shape[0]
    kinds = 2 * reach + 1
    field[...] = (val[...] * cond[...]).reshape(xs * num_val, plane)
    step = dot3(field[...], plane_h[...], plane_l[...])
    real, imag = step[:, :count], step[:, count:]
    size = kinds * num_val
    cos_h, sin_h, cos_l, sin_l = line_h[0], line_h[1], line_l[0], line_l[1]
    picked[:size, :] = dot3_left(cos_h, cos_l, real) + dot3_left(sin_h, sin_l, imag)
    picked[size:, :] = dot3_left(cos_h, cos_l, imag) - dot3_left(sin_h, sin_l, real)
    source = picked[...].astype(jnp.bfloat16)
    first, second = codes[:, 0:1], codes[:, 1:2]

    def body(t, carry):
        here = pl.ds(pl.multiple_of(t * tile, tile), tile)
        index = gmap[:, here]
        kx = index // (GRID * GRID)
        code = index % (GRID * GRID)
        ky, kz = code // GRID, code % GRID
        kx = jnp.where(kx < GRID // 2, kx, kx - GRID)
        direct = ((kz > 0) & (kz < GRID // 2)) | ((kz == 0) & (ky < GRID // 2))
        kx = jnp.where(direct, kx, -kx) + reach
        sign = jnp.where(direct, 1.0, -1.0).astype(jnp.float32)
        hit = (code == first) | (code == second)
        columns = dot(source, jnp.where(hit, 1.0, 0.0).astype(jnp.bfloat16))
        columns = columns.reshape(2, kinds, num_val, tile)
        real = jnp.zeros((num_val, tile), jnp.float32)
        imag = jnp.zeros((num_val, tile), jnp.float32)
        for k in range(kinds):
            keep = jnp.broadcast_to(kx == k, (num_val, tile))
            real = jnp.where(keep, columns[0, k], real)
            imag = jnp.where(keep, columns[1, k], imag)
        out[:, here] = jnp.concatenate([real, imag * sign], axis=0).astype(jnp.bfloat16)
        return carry

    lax.fori_loop(0, out.shape[1] // tile, body, 0)


def transform_pairs(val, cond, gmap):
    xs, num_val, plane = val.shape
    waves = gmap.shape[1]
    table, codes, line, reach = tables(waves, num_val)
    plane_h, plane_l = np_halves(table)
    line_h, line_l = np_halves(line)
    count = codes.shape[0]
    operands = (val, cond, plane_h, plane_l, line_h, line_l, codes, gmap)
    held = [pltpu.VMEM(x.shape, x.dtype) for x in operands]
    return pl.pallas_call(
        functools.partial(pair_kernel, reach, min(512, waves)),
        out_shape=jax.ShapeDtypeStruct((2 * num_val, waves), jnp.bfloat16),
        in_specs=[pl.BlockSpec(memory_space=pl.ANY)] * 8,
        out_specs=pl.BlockSpec(memory_space=VMEM),
        scratch_shapes=[
            pltpu.VMEM((xs * num_val, plane), jnp.float32),
            pltpu.VMEM((2 * (2 * reach + 1) * num_val, count), jnp.float32),
        ]
        + held
        + [pltpu.SemaphoreType.DMA((8,))],
        compiler_params=pltpu.CompilerParams(vmem_limit_bytes=62 << 20),
    )(*[jnp.asarray(x) for x in operands])


def chi_kernel(num_cond, num_val, scalars, rows, columns, out, scaled):
    num = out.shape[0]

    @pl.when(pl.program_id(0) == 0)
    def _():
        depth = rows.shape[0]
        lane = lax.broadcasted_iota(jnp.int32, (1, depth), 1)
        band, orbital = lane // (2 * num_val), lane % num_val

        def pick(first, count, where):
            def step(i, held):
                return jnp.where(where == i, scalars[first + i], held)

            return lax.fori_loop(0, count, step, jnp.zeros((1, depth), jnp.float32))

        gap = pick(0, num_cond, band) - pick(num_cond, num_val, orbital)
        norm = math.sqrt(num_cond * num_val)
        turned = rows[...].astype(jnp.float32).T
        for w in range(num):
            omega = scalars[num_cond + num_val + w]
            weight = -2.0 * gap / (gap * gap + omega * omega) / norm
            scaled[w] = (turned * weight).astype(jnp.bfloat16)

    for w in range(num):
        out[w] = dot(scaled[w], columns[...])


def chi_of(eps_cond, eps_val, omega, rows, columns):
    depth, row_width = rows.shape
    width = columns.shape[1]
    num = omega.shape[0]
    tile = min(512, width)
    grant = 4 * depth * (row_width + tile) + 8 * num * row_width * tile
    grant += (2 * num + 12) * row_width * depth + (8 << 20)
    scalars = jnp.concatenate([eps_cond, eps_val, omega])
    return pl.pallas_call(
        functools.partial(chi_kernel, eps_cond.shape[0], eps_val.shape[0]),
        grid=(width // tile,),
        out_shape=jax.ShapeDtypeStruct((num, row_width, width), jnp.float32),
        in_specs=[pl.BlockSpec(memory_space=SMEM)]
        + [
            pl.BlockSpec((depth, row_width), lambda c: (0, 0)),
            pl.BlockSpec((depth, tile), lambda c: (0, c)),
        ],
        out_specs=pl.BlockSpec((num, row_width, tile), lambda c: (0, 0, c)),
        scratch_shapes=[pltpu.VMEM((num, row_width, depth), jnp.bfloat16)],
        compiler_params=pltpu.CompilerParams(vmem_limit_bytes=grant),
    )(scalars, rows, columns)


def body(valence, conduction, eps_val, eps_cond, omega, gmap):
    wide, narrow = lax.axis_size("wide"), lax.axis_size("narrow")
    devices = wide * narrow
    num_val, chunk = valence.shape
    num_local = conduction.shape[0]
    assert num_local == 1
    plane = GRID * GRID
    waves = gmap.shape[0]
    [full] = gather(valence, wide, narrow, 0, 0, 0)
    if chunk != plane:
        full = full.reshape(GRID, devices // GRID, num_val, chunk)
        full = jnp.transpose(full, (0, 2, 1, 3)).reshape(GRID, num_val, plane)
    local = transform_pairs(full, conduction.reshape(GRID, 1, plane), gmap.reshape(1, waves))
    columns, rows = gather(local, wide, narrow, waves // narrow, waves // wide, 1)
    depth = devices * 2 * num_val
    columns = columns.reshape(depth, waves // narrow)
    rows = rows.reshape(depth, waves // wide)
    return chi_of(eps_cond, eps_val, omega, rows, columns)


def solution(mesh):
    placed = (P(None, ("wide", "narrow")), P(("wide", "narrow"), None), P(), P(), P(), P())
    return jax.shard_map(
        body, mesh=mesh, in_specs=placed, out_specs=P(None, "wide", "narrow"), check_vma=False
    )
```

```python
import functools
import math

import jax
import jax.numpy as jnp
import numpy as np
from jax import lax
from jax.experimental import pallas as pl
from jax.experimental.pallas import tpu as pltpu
from jax.sharding import PartitionSpec as P

GRID = 32
MESH = pl.DeviceIdType.MESH
VMEM = pltpu.MemorySpace.VMEM
HBM = pltpu.MemorySpace.HBM
SMEM = pltpu.MemorySpace.SMEM


def wide_factors(wide):
    chips = wide // 2
    inner = 2 ** (int(math.log2(chips)) // 2)
    return chips // inner, inner


def gather_kernel(wide, narrow, split, row_width, row_step, src, out, *rest):
    if row_width:
        rows, send_sem, recv_sem, own_sem, row_send, row_recv = rest
    else:
        send_sem, recv_sem, own_sem = rest
    outer, inner = wide_factors(wide)
    w, n = lax.axis_index("wide"), lax.axis_index("narrow")
    core = lax.rem(w, 2)
    y = lax.rem(w // 2, inner)
    z = w // (2 * inner)

    def wide_at(zz, yy, cc):
        return (zz * inner + yy) * 2 + cc

    def slot(zz, yy, cc, nn):
        return wide_at(zz, yy, cc) * narrow + nn

    xs = [lax.rem(n + i, narrow) for i in range(1, narrow)]
    zs = [lax.rem(z + i, outer) for i in range(1, outer)]
    ys = [lax.rem(y + i, inner) for i in range(1, inner)]
    to_x = [(w, nn) for nn in xs]
    to_z = [(wide_at(zz, y, core), n) for zz in zs]
    to_y = [(wide_at(z, yy, core), n) for yy in ys]
    to_core = [(wide_at(z, y, 1 - core), n)]
    peers = to_x + to_z + to_y + to_core

    barrier = pltpu.get_barrier_semaphore()
    for peer in peers:
        pl.semaphore_signal(barrier, inc=1, device_id=peer, device_id_type=MESH)
    pl.semaphore_wait(barrier, len(peers))

    def piece(nn):
        if split:
            return src.at[:, pl.ds(pl.multiple_of(nn * split, split), split)]
        return src

    started = []

    def send(ref, index, target):
        copy = pltpu.make_async_remote_copy(
            src_ref=ref,
            dst_ref=out.at[index],
            send_sem=send_sem.at[len(started)],
            recv_sem=recv_sem.at[index],
            device_id=target,
            device_id_type=MESH,
        )
        copy.start()
        started.append(copy)

    def arrived(index):
        pltpu.make_async_remote_copy(
            src_ref=out.at[index],
            dst_ref=out.at[index],
            send_sem=send_sem.at[0],
            recv_sem=recv_sem.at[index],
            device_id=to_core[0],
            device_id_type=MESH,
        ).wait_recv()

    mine = slot(z, y, core, n)
    for target in to_x:
        send(piece(target[1]), mine, target)
    for target in to_z + to_y + to_core:
        send(piece(n), mine, target)
    own = pltpu.make_async_copy(piece(n), out.at[mine], own_sem)
    own.start()
    for nn in xs:
        index = slot(z, y, core, nn)
        arrived(index)
        for target in to_z + to_y + to_core:
            send(out.at[index], index, target)
    for zz in zs:
        for nn in [n] + xs:
            index = slot(zz, y, core, nn)
            arrived(index)
            for target in to_y + to_core:
                send(out.at[index], index, target)
    for yy in ys:
        for zz in [z] + zs:
            for nn in [n] + xs:
                index = slot(zz, yy, core, nn)
                arrived(index)
                send(out.at[index], index, to_core[0])
    own.wait()

    if row_width:
        holder = w // (wide // narrow)
        first = pl.multiple_of(lax.rem(w, wide // narrow) * row_step, 128)
        group = 2 * narrow

    def row_copy(index, target, start, sem):
        return pltpu.make_async_remote_copy(
            src_ref=out.at[pl.ds(start, group), :, pl.ds(first, row_width)],
            dst_ref=rows.at[pl.ds(start, group)],
            send_sem=row_send.at[sem],
            recv_sem=row_recv.at[index],
            device_id=target,
            device_id_type=MESH,
        )

    chips = [(zz, yy) for yy in [y] + ys for zz in [z] + zs]
    for number, (zz, yy) in enumerate(chips):
        for nn in [n] + xs:
            arrived(slot(zz, yy, 1 - core, nn))
        if row_width:
            @pl.when(n == holder)
            def _():
                for k, target in enumerate(to_x):
                    row_copy(number, target, slot(zz, yy, 0, 0), number * len(to_x) + k).start()

    for copy in started:
        copy.wait_send()
    if row_width:
        @pl.when(n == holder)
        def _():
            rows[...] = out[:, :, pl.ds(first, row_width)]
            for number, (zz, yy) in enumerate(chips):
                for k, target in enumerate(to_x):
                    row_copy(number, target, slot(zz, yy, 0, 0), number * len(to_x) + k).wait_send()

        @pl.when(n != holder)
        def _():
            for number, (zz, yy) in enumerate(chips):
                row_copy(number, to_x[0], slot(zz, yy, 0, 0), 0).wait_recv()


def gather(src, wide, narrow, split, row_width, row_step, collective_id):
    outer, inner = wide_factors(wide)
    devices = wide * narrow
    n_x, n_z, n_y = narrow - 1, outer - 1, inner - 1
    sends = n_x + n_z + n_y + 1
    sends += n_x * (n_z + n_y + 1) + n_z * narrow * (n_y + 1) + n_y * outer * narrow
    block = (src.shape[0], split or src.shape[1])
    out_shape = [jax.ShapeDtypeStruct((devices,) + block, src.dtype)]
    scratch = [
        pltpu.SemaphoreType.DMA((sends,)),
        pltpu.SemaphoreType.DMA((devices,)),
        pltpu.SemaphoreType.DMA,
    ]
    if row_width:
        out_shape.append(jax.ShapeDtypeStruct((devices, src.shape[0], row_width), src.dtype))
        scratch.append(pltpu.SemaphoreType.DMA((outer * inner * n_x,)))
        scratch.append(pltpu.SemaphoreType.DMA((outer * inner,)))
    return pl.pallas_call(
        functools.partial(gather_kernel, wide, narrow, split, row_width, row_step),
        out_shape=out_shape,
        in_specs=[pl.BlockSpec(memory_space=pl.ANY)],
        out_specs=[pl.BlockSpec(memory_space=VMEM if row_width else pl.ANY)] * len(out_shape),
        scratch_shapes=scratch,
        compiler_params=pltpu.CompilerParams(
            collective_id=collective_id, has_side_effects=True, vmem_limit_bytes=(48 if row_width else 63) << 20
        ),
    )(src)


@functools.lru_cache(None)
def tables(num_waves, num_val):
    fold = np.arange(GRID)
    fold = np.where(fold < GRID // 2, fold, fold - GRID)
    squares = fold**2
    lengths = (squares[:, None, None] + squares[None, :, None] + squares[None, None, :]).reshape(-1)
    limit = int(np.sort(lengths)[num_waves - 1])
    reach = math.isqrt(limit)
    assert reach < GRID // 2
    half = [
        (ky, kz)
        for ky in range(-reach, reach + 1)
        for kz in range(0, reach + 1)
        if ky * ky + kz * kz <= limit and (kz > 0 or ky >= 0)
    ]
    count = -(-len(half) // 128) * 128
    kys = np.array([k for k, _ in half])
    kzs = np.array([k for _, k in half])
    points = np.arange(GRID)
    turn = 2.0 * np.pi / GRID
    phase = (points[:, None, None] * kys + points[None, :, None] * kzs) % GRID
    phase = phase.reshape(GRID * GRID, len(half)) * turn
    plane = np.zeros((GRID * GRID, 2 * count))
    plane[:, : len(half)] = np.cos(phase)
    plane[:, count : count + len(half)] = -np.sin(phase)
    codes = np.full((count, 2), -1, np.int32)
    codes[: len(half), 0] = (kys % GRID) * GRID + kzs % GRID
    codes[: len(half), 1] = (-kys % GRID) * GRID + -kzs % GRID
    kxs = np.arange(-reach, reach + 1)
    line = (kxs[:, None] * points[None, :] % GRID) * turn
    eye = np.eye(num_val)
    norm = 1.0 / math.sqrt(GRID**3)
    cosine = np.kron(np.cos(line), eye) * norm
    sine = np.kron(np.sin(line), eye) * norm
    return plane, codes, np.stack([cosine, sine]), reach


MARGIN = 128


def window(tile):
    return tile // 2 + 2 * MARGIN


@functools.lru_cache(None)
def half_lists(num_waves, narrow, tiles):
    fold = np.arange(GRID)
    fold = np.where(fold < GRID // 2, fold, fold - GRID)
    kx, ky, kz = [k.reshape(-1) for k in np.meshgrid(fold, fold, fold, indexing="ij")]
    lengths = kx * kx + ky * ky + kz * kz
    ordered = np.sort(lengths)[:num_waves]
    half = (kz > 0) | ((kz == 0) & ((ky > 0) | ((ky == 0) & (kx >= 0))))
    chosen = np.nonzero(half & (lengths <= ordered[-1]))[0]
    chosen = chosen[np.argsort(lengths[chosen], kind="stable")]
    sizes = lengths[chosen]
    part = num_waves // narrow
    slots = part // 2 + 2 * MARGIN
    lists = np.full((narrow, 1, slots), -1, np.int32)
    for n in range(narrow):
        begin = np.searchsorted(sizes, ordered[n * part])
        end = np.searchsorted(sizes, ordered[(n + 1) * part - 1], side="right")
        assert end - begin + MARGIN <= slots
        lists[n, 0, MARGIN : MARGIN + end - begin] = chosen[begin:end]
        for tile in tiles:
            for t in range(part // tile):
                g = n * part + t * tile
                low = np.searchsorted(sizes, ordered[g]) - begin + MARGIN
                high = np.searchsorted(sizes, ordered[g + tile - 1], side="right") - begin + MARGIN
                assert t * tile // 2 <= low and high <= t * tile // 2 + window(tile)
    return lists


def np_halves(table):
    table = np.asarray(table, np.float32)
    high = table.astype(jnp.bfloat16)
    return high, (table - high.astype(np.float32)).astype(jnp.bfloat16)


def split_bf16(x):
    high = x.astype(jnp.bfloat16)
    return high, (x - high.astype(jnp.float32)).astype(jnp.bfloat16)


def dot(a, b):
    return jnp.dot(a, b, preferred_element_type=jnp.float32)


def dot3(a, b_high, b_low):
    a_high, a_low = split_bf16(a)
    return dot(a_high, b_high) + (dot(a_low, b_high) + dot(a_high, b_low))


def dot3_left(a_high, a_low, b):
    b_high, b_low = split_bf16(b)
    return dot(a_high, b_high) + (dot(a_high, b_low) + dot(a_low, b_high))


def pair_kernel(reach, tile, *refs):
    sources, out, field, picked = refs[:8], refs[8], refs[9], refs[10]
    held, sems = refs[11:19], refs[19]
    copies = [pltpu.make_async_copy(a, b, sems.at[i]) for i, (a, b) in enumerate(zip(sources, held))]
    for copy in copies:
        copy.start()
    val, cond, plane_h, plane_l, line_h, line_l, codes, gmap = held
    for copy in copies:
        copy.wait()
    xs, num_val, plane = val.shape
    count = codes.shape[0]
    kinds = 2 * reach + 1
    field[...] = (val[...] * cond[...]).reshape(xs * num_val, plane)
    step = dot3(field[...], plane_h[...], plane_l[...])
    real, imag = step[:, :count], step[:, count:]
    size = kinds * num_val
    cos_h, sin_h, cos_l, sin_l = line_h[0], line_h[1], line_l[0], line_l[1]
    picked[:size, :] = dot3_left(cos_h, cos_l, real) + dot3_left(sin_h, sin_l, imag)
    picked[size:, :] = dot3_left(cos_h, cos_l, imag) - dot3_left(sin_h, sin_l, real)
    source = picked[...].astype(jnp.bfloat16)
    first, second = codes[:, 0:1], codes[:, 1:2]

    def body(t, carry):
        here = pl.ds(pl.multiple_of(t * tile, tile), tile)
        index = gmap[:, here]
        kx = index // (GRID * GRID)
        code = index % (GRID * GRID)
        ky, kz = code // GRID, code % GRID
        kx = jnp.where(kx < GRID // 2, kx, kx - GRID)
        direct = ((kz > 0) & (kz < GRID // 2)) | ((kz == 0) & (ky < GRID // 2))
        kx = jnp.where(direct, kx, -kx) + reach
        sign = jnp.where(direct, 1.0, -1.0).astype(jnp.float32)
        hit = (code == first) | (code == second)
        columns = dot(source, jnp.where(hit, 1.0, 0.0).astype(jnp.bfloat16))
        columns = columns.reshape(2, kinds, num_val, tile)
        real = jnp.zeros((num_val, tile), jnp.float32)
        imag = jnp.zeros((num_val, tile), jnp.float32)
        for k in range(kinds):
            keep = jnp.broadcast_to(kx == k, (num_val, tile))
            real = jnp.where(keep, columns[0, k], real)
            imag = jnp.where(keep, columns[1, k], imag)
        out[:, here] = jnp.concatenate([real, imag * sign], axis=0).astype(jnp.bfloat16)
        return carry

    lax.fori_loop(0, out.shape[1] // tile, body, 0)


def transform_pairs(val, cond, gmap, num_waves):
    xs, num_val, plane = val.shape
    waves = gmap.shape[1]
    table, codes, line, reach = tables(num_waves, num_val)
    plane_h, plane_l = np_halves(table)
    line_h, line_l = np_halves(line)
    count = codes.shape[0]
    operands = (val, cond, plane_h, plane_l, line_h, line_l, codes, gmap)
    held = [pltpu.VMEM(x.shape, x.dtype) for x in operands]
    return pl.pallas_call(
        functools.partial(pair_kernel, reach, 256),
        out_shape=jax.ShapeDtypeStruct((2 * num_val, waves), jnp.bfloat16),
        in_specs=[pl.BlockSpec(memory_space=pl.ANY)] * 8,
        out_specs=pl.BlockSpec(memory_space=VMEM),
        scratch_shapes=[
            pltpu.VMEM((xs * num_val, plane), jnp.float32),
            pltpu.VMEM((2 * (2 * reach + 1) * num_val, count), jnp.float32),
        ]
        + held
        + [pltpu.SemaphoreType.DMA((8,))],
        compiler_params=pltpu.CompilerParams(vmem_limit_bytes=62 << 20),
    )(*[jnp.asarray(x) for x in operands])


def expand(held, listed, index, num_val):
    depth, slots = held.shape
    tile = index.shape[1]
    area = GRID * GRID
    lx, ly, lz = listed // area, listed // GRID % GRID, listed % GRID
    mirror = (GRID - lx) % GRID * area + (GRID - ly) % GRID * GRID + (GRID - lz) % GRID
    mirror = jnp.where(listed < 0, -1, mirror)

    def column(row):
        turned = jnp.broadcast_to(row, (128, slots)).T
        return jnp.concatenate([turned] * (tile // 128), axis=1)

    hit = (index == column(listed)) | (index == column(mirror))
    values = dot(held, jnp.where(hit, 1.0, 0.0).astype(jnp.bfloat16))
    kx, ky, kz = index // area, index // GRID % GRID, index % GRID
    low = GRID // 2
    direct = ((kz > 0) & (kz < low)) | (
        (kz == 0) & (((ky > 0) & (ky < low)) | ((ky == 0) & (kx < low)))
    )
    sign = jnp.where(direct, 1.0, -1.0).astype(jnp.float32)
    row = lax.broadcasted_iota(jnp.int32, (depth, tile), 0)
    return values * jnp.where(row // num_val % 2 == 1, sign, 1.0)


def chi_kernel(num_cond, num_val, scalars, gmap, lists, rows, columns, out, scaled):
    num, row_width, tile = out.shape
    depth = rows.shape[0]
    narrow, wide = lists.shape[0], gmap.shape[1] // row_width
    w, n = lax.axis_index("wide"), lax.axis_index("narrow")
    step = pl.program_id(0)

    @pl.when(step == 0)
    def _():
        lane = lax.broadcasted_iota(jnp.int32, (1, depth), 1)
        band, orbital = lane // (2 * num_val), lane % num_val

        def pick(first, count, where):
            def select(i, held):
                return jnp.where(where == i, scalars[first + i], held)

            return lax.fori_loop(0, count, select, jnp.zeros((1, depth), jnp.float32))

        gap = pick(0, num_cond, band) - pick(num_cond, num_val, orbital)
        norm = math.sqrt(num_cond * num_val)
        first = pl.multiple_of(lax.rem(w, wide // narrow) * (row_width // 2), 128)
        listed = lists[w // (wide // narrow), :, pl.ds(first, rows.shape[1])]
        index = gmap[:, pl.ds(pl.multiple_of(w * row_width, 128), row_width)]
        turned = expand(rows[...], listed, index, num_val).T
        for i in range(num):
            omega = scalars[num_cond + num_val + i]
            weight = -2.0 * gap / (gap * gap + omega * omega) / norm
            scaled[i] = (turned * weight).astype(jnp.bfloat16)

    first = pl.multiple_of(step * (tile // 2), 128)
    here = pl.ds(first, window(tile))
    part = gmap.shape[1] // narrow
    index = gmap[:, pl.ds(pl.multiple_of(n * part + step * tile, 128), tile)]
    panel = expand(columns[:, here], lists[n, :, here], index, num_val).astype(jnp.bfloat16)
    for i in range(num):
        out[i] = dot(scaled[i], panel)


def chi_of(eps_cond, eps_val, omega, gmap, lists, rows, columns, row_width, width):
    depth, row_slots = rows.shape
    num = omega.shape[0]
    tile = min(512, width)
    grant = 4 * depth * (row_slots + columns.shape[1]) + 8 * num * row_width * tile
    grant += (2 * num + 16) * row_width * depth + 16 * depth * tile + (8 << 20)
    scalars = jnp.concatenate([eps_cond, eps_val, omega])
    return pl.pallas_call(
        functools.partial(chi_kernel, eps_cond.shape[0], eps_val.shape[0]),
        grid=(width // tile,),
        out_shape=jax.ShapeDtypeStruct((num, row_width, width), jnp.float32),
        in_specs=[
            pl.BlockSpec(memory_space=SMEM),
            pl.BlockSpec(gmap.shape, lambda c: (0, 0)),
            pl.BlockSpec(lists.shape, lambda c: (0, 0, 0)),
            pl.BlockSpec(rows.shape, lambda c: (0, 0)),
            pl.BlockSpec(columns.shape, lambda c: (0, 0)),
        ],
        out_specs=pl.BlockSpec((num, row_width, tile), lambda c: (0, 0, c)),
        scratch_shapes=[pltpu.VMEM((num, row_width, depth), jnp.bfloat16)],
        compiler_params=pltpu.CompilerParams(vmem_limit_bytes=min(grant, 60 << 20)),
    )(scalars, gmap, jnp.asarray(lists), rows, columns)


def body(valence, conduction, eps_val, eps_cond, omega, gmap):
    wide, narrow = lax.axis_size("wide"), lax.axis_size("narrow")
    devices = wide * narrow
    num_val, chunk = valence.shape
    num_local = conduction.shape[0]
    assert num_local == 1
    plane = GRID * GRID
    waves = gmap.shape[0]
    [full] = gather(valence, wide, narrow, 0, 0, 0, 0)
    if chunk != plane:
        full = full.reshape(GRID, devices // GRID, num_val, chunk)
        full = jnp.transpose(full, (0, 2, 1, 3)).reshape(GRID, num_val, plane)
    row_width, width = waves // wide, waves // narrow
    lists = half_lists(waves, narrow, (row_width, min(512, width)))
    wanted = np.maximum(lists.reshape(1, -1), 0)
    local = transform_pairs(full, conduction.reshape(GRID, 1, plane), wanted, waves)
    slots, row_slots = lists.shape[2], window(row_width)
    columns, rows = gather(local, wide, narrow, slots, row_slots, row_width // 2, 1)
    depth = devices * 2 * num_val
    columns, rows = columns.reshape(depth, slots), rows.reshape(depth, row_slots)
    spot = gmap.reshape(1, waves)
    return chi_of(eps_cond, eps_val, omega, spot, lists, rows, columns, row_width, width)


def solution(mesh):
    placed = (P(None, ("wide", "narrow")), P(("wide", "narrow"), None), P(), P(), P(), P())
    return jax.shard_map(
        body, mesh=mesh, in_specs=placed, out_specs=P(None, "wide", "narrow"), check_vma=False
    )
```

```python
import functools
import math

import jax
import jax.numpy as jnp
import numpy as np
from jax import lax
from jax.experimental import pallas as pl
from jax.experimental.pallas import tpu as pltpu
from jax.sharding import PartitionSpec as P

GRID = 32
MESH = pl.DeviceIdType.MESH
VMEM = pltpu.MemorySpace.VMEM
HBM = pltpu.MemorySpace.HBM
SMEM = pltpu.MemorySpace.SMEM


def wide_factors(wide):
    chips = wide // 2
    inner = 2 ** (int(math.log2(chips)) // 2)
    return chips // inner, inner


def gather_kernel(wide, narrow, split, row_width, row_step, src, out, *rest):
    if row_width:
        rows, send_sem, recv_sem, own_sem, row_send, row_recv = rest
    else:
        send_sem, recv_sem, own_sem = rest
    outer, inner = wide_factors(wide)
    w, n = lax.axis_index("wide"), lax.axis_index("narrow")
    core = lax.rem(w, 2)
    y = lax.rem(w // 2, inner)
    z = w // (2 * inner)

    def wide_at(zz, yy, cc):
        return (zz * inner + yy) * 2 + cc

    def slot(zz, yy, cc, nn):
        return wide_at(zz, yy, cc) * narrow + nn

    xs = [lax.rem(n + i, narrow) for i in range(1, narrow)]
    zs = [lax.rem(z + i, outer) for i in range(1, outer)]
    ys = [lax.rem(y + i, inner) for i in range(1, inner)]
    to_x = [(w, nn) for nn in xs]
    to_z = [(wide_at(zz, y, core), n) for zz in zs]
    to_y = [(wide_at(z, yy, core), n) for yy in ys]
    to_core = [(wide_at(z, y, 1 - core), n)]
    peers = to_x + to_z + to_y + to_core

    barrier = pltpu.get_barrier_semaphore()
    for peer in peers:
        pl.semaphore_signal(barrier, inc=1, device_id=peer, device_id_type=MESH)
    pl.semaphore_wait(barrier, len(peers))

    def piece(nn):
        if split:
            return src.at[:, pl.ds(pl.multiple_of(nn * split, split), split)]
        return src

    started = []

    def send(ref, index, target):
        copy = pltpu.make_async_remote_copy(
            src_ref=ref,
            dst_ref=out.at[index],
            send_sem=send_sem.at[len(started)],
            recv_sem=recv_sem.at[index],
            device_id=target,
            device_id_type=MESH,
        )
        copy.start()
        started.append(copy)

    def arrived(index):
        pltpu.make_async_remote_copy(
            src_ref=out.at[index],
            dst_ref=out.at[index],
            send_sem=send_sem.at[0],
            recv_sem=recv_sem.at[index],
            device_id=to_core[0],
            device_id_type=MESH,
        ).wait_recv()

    if row_width:
        holder = w // (wide // narrow)
        first = pl.multiple_of(lax.rem(w, wide // narrow) * row_step, 128)
        group = 2 * narrow

    def row_copy(index, target, start, sem):
        return pltpu.make_async_remote_copy(
            src_ref=out.at[pl.ds(start, group), :, pl.ds(first, row_width)],
            dst_ref=rows.at[pl.ds(start, group)],
            send_sem=row_send.at[sem],
            recv_sem=row_recv.at[index],
            device_id=target,
            device_id_type=MESH,
        )

    chips = [(zz, yy) for yy in [y] + ys for zz in [z] + zs]

    def finish(number):
        zz, yy = chips[number]
        for nn in [n] + xs:
            arrived(slot(zz, yy, 1 - core, nn))
        if row_width:
            @pl.when(n == holder)
            def _():
                for k, target in enumerate(to_x):
                    row_copy(number, target, slot(zz, yy, 0, 0), number * len(to_x) + k).start()

    mine = slot(z, y, core, n)
    for target in to_x:
        send(piece(target[1]), mine, target)
    for target in to_z + to_y + to_core:
        send(piece(n), mine, target)
    own = pltpu.make_async_copy(piece(n), out.at[mine], own_sem)
    own.start()
    for nn in xs:
        index = slot(z, y, core, nn)
        arrived(index)
        for target in to_z + to_y + to_core:
            send(out.at[index], index, target)
    for zz in zs:
        for nn in [n] + xs:
            index = slot(zz, y, core, nn)
            arrived(index)
            for target in to_y + to_core:
                send(out.at[index], index, target)
    own.wait()
    for number in range(outer):
        finish(number)
    for number, (zz, yy) in enumerate(chips[outer:], outer):
        for nn in [n] + xs:
            index = slot(zz, yy, core, nn)
            arrived(index)
            send(out.at[index], index, to_core[0])
        if number > outer:
            finish(number - 1)
    if len(chips) > outer:
        finish(len(chips) - 1)

    for copy in started:
        copy.wait_send()
    if row_width:
        @pl.when(n == holder)
        def _():
            rows[...] = out[:, :, pl.ds(first, row_width)]
            for number, (zz, yy) in enumerate(chips):
                for k, target in enumerate(to_x):
                    row_copy(number, target, slot(zz, yy, 0, 0), number * len(to_x) + k).wait_send()

        @pl.when(n != holder)
        def _():
            for number, (zz, yy) in enumerate(chips):
                row_copy(number, to_x[0], slot(zz, yy, 0, 0), 0).wait_recv()


def gather(src, wide, narrow, split, row_width, row_step, collective_id):
    outer, inner = wide_factors(wide)
    devices = wide * narrow
    n_x, n_z, n_y = narrow - 1, outer - 1, inner - 1
    sends = n_x + n_z + n_y + 1
    sends += n_x * (n_z + n_y + 1) + n_z * narrow * (n_y + 1) + n_y * outer * narrow
    block = (src.shape[0], split or src.shape[1])
    out_shape = [jax.ShapeDtypeStruct((devices,) + block, src.dtype)]
    scratch = [
        pltpu.SemaphoreType.DMA((sends,)),
        pltpu.SemaphoreType.DMA((devices,)),
        pltpu.SemaphoreType.DMA,
    ]
    if row_width:
        out_shape.append(jax.ShapeDtypeStruct((devices, src.shape[0], row_width), src.dtype))
        scratch.append(pltpu.SemaphoreType.DMA((outer * inner * n_x,)))
        scratch.append(pltpu.SemaphoreType.DMA((outer * inner,)))
    return pl.pallas_call(
        functools.partial(gather_kernel, wide, narrow, split, row_width, row_step),
        out_shape=out_shape,
        in_specs=[pl.BlockSpec(memory_space=pl.ANY)],
        out_specs=[pl.BlockSpec(memory_space=VMEM if row_width else pl.ANY)] * len(out_shape),
        scratch_shapes=scratch,
        compiler_params=pltpu.CompilerParams(
            collective_id=collective_id, has_side_effects=True, vmem_limit_bytes=(48 if row_width else 63) << 20
        ),
    )(src)


@functools.lru_cache(None)
def tables(num_waves, num_val):
    fold = np.arange(GRID)
    fold = np.where(fold < GRID // 2, fold, fold - GRID)
    squares = fold**2
    lengths = (squares[:, None, None] + squares[None, :, None] + squares[None, None, :]).reshape(-1)
    limit = int(np.sort(lengths)[num_waves - 1])
    reach = math.isqrt(limit)
    assert reach < GRID // 2
    half = [
        (ky, kz)
        for ky in range(-reach, reach + 1)
        for kz in range(0, reach + 1)
        if ky * ky + kz * kz <= limit and (kz > 0 or ky >= 0)
    ]
    count = -(-len(half) // 128) * 128
    kys = np.array([k for k, _ in half])
    kzs = np.array([k for _, k in half])
    points = np.arange(GRID)
    turn = 2.0 * np.pi / GRID
    phase = (points[:, None, None] * kys + points[None, :, None] * kzs) % GRID
    phase = phase.reshape(GRID * GRID, len(half)) * turn
    plane = np.zeros((GRID * GRID, 2 * count))
    plane[:, : len(half)] = np.cos(phase)
    plane[:, count : count + len(half)] = -np.sin(phase)
    codes = np.full((count, 2), -1, np.int32)
    codes[: len(half), 0] = (kys % GRID) * GRID + kzs % GRID
    codes[: len(half), 1] = (-kys % GRID) * GRID + -kzs % GRID
    kxs = np.arange(-reach, reach + 1)
    line = (kxs[:, None] * points[None, :] % GRID) * turn
    eye = np.eye(num_val)
    norm = 1.0 / math.sqrt(GRID**3)
    cosine = np.kron(np.cos(line), eye) * norm
    sine = np.kron(np.sin(line), eye) * norm
    return plane, codes, np.stack([cosine, sine]), reach


MARGIN = 128


def window(tile):
    return tile // 2 + 2 * MARGIN


@functools.lru_cache(None)
def half_lists(num_waves, narrow, tiles):
    fold = np.arange(GRID)
    fold = np.where(fold < GRID // 2, fold, fold - GRID)
    kx, ky, kz = [k.reshape(-1) for k in np.meshgrid(fold, fold, fold, indexing="ij")]
    lengths = kx * kx + ky * ky + kz * kz
    ordered = np.sort(lengths)[:num_waves]
    half = (kz > 0) | ((kz == 0) & ((ky > 0) | ((ky == 0) & (kx >= 0))))
    chosen = np.nonzero(half & (lengths <= ordered[-1]))[0]
    chosen = chosen[np.argsort(lengths[chosen], kind="stable")]
    sizes = lengths[chosen]
    part = num_waves // narrow
    slots = part // 2 + 2 * MARGIN
    lists = np.full((narrow, 1, slots), -1, np.int32)
    for n in range(narrow):
        begin = np.searchsorted(sizes, ordered[n * part])
        end = np.searchsorted(sizes, ordered[(n + 1) * part - 1], side="right")
        assert end - begin + MARGIN <= slots
        lists[n, 0, MARGIN : MARGIN + end - begin] = chosen[begin:end]
        for tile in tiles:
            for t in range(part // tile):
                g = n * part + t * tile
                low = np.searchsorted(sizes, ordered[g]) - begin + MARGIN
                high = np.searchsorted(sizes, ordered[g + tile - 1], side="right") - begin + MARGIN
                assert t * tile // 2 <= low and high <= t * tile // 2 + window(tile)
    return lists


def np_halves(table):
    table = np.asarray(table, np.float32)
    high = table.astype(jnp.bfloat16)
    return high, (table - high.astype(np.float32)).astype(jnp.bfloat16)


def split_bf16(x):
    high = x.astype(jnp.bfloat16)
    return high, (x - high.astype(jnp.float32)).astype(jnp.bfloat16)


def dot(a, b):
    return jnp.dot(a, b, preferred_element_type=jnp.float32)


def dot3(a, b_high, b_low):
    a_high, a_low = split_bf16(a)
    return dot(a_high, b_high) + (dot(a_low, b_high) + dot(a_high, b_low))


def dot3_left(a_high, a_low, b):
    b_high, b_low = split_bf16(b)
    return dot(a_high, b_high) + (dot(a_high, b_low) + dot(a_low, b_high))


def pair_kernel(reach, tile, *refs):
    sources, out, field, picked = refs[:8], refs[8], refs[9], refs[10]
    held, sems = refs[11:19], refs[19]
    copies = [pltpu.make_async_copy(a, b, sems.at[i]) for i, (a, b) in enumerate(zip(sources, held))]
    for copy in copies:
        copy.start()
    val, cond, plane_h, plane_l, line_h, line_l, codes, gmap = held
    for copy in copies:
        copy.wait()
    xs, num_val, plane = val.shape
    count = codes.shape[0]
    kinds = 2 * reach + 1
    field[...] = (val[...] * cond[...]).reshape(xs * num_val, plane)
    step = dot3(field[...], plane_h[...], plane_l[...])
    real, imag = step[:, :count], step[:, count:]
    size = kinds * num_val
    cos_h, sin_h, cos_l, sin_l = line_h[0], line_h[1], line_l[0], line_l[1]
    picked[:size, :] = dot3_left(cos_h, cos_l, real) + dot3_left(sin_h, sin_l, imag)
    picked[size:, :] = dot3_left(cos_h, cos_l, imag) - dot3_left(sin_h, sin_l, real)
    source = picked[...].astype(jnp.bfloat16)
    first, second = codes[:, 0:1], codes[:, 1:2]

    def body(t, carry):
        here = pl.ds(pl.multiple_of(t * tile, tile), tile)
        index = gmap[:, here]
        kx = index // (GRID * GRID)
        code = index % (GRID * GRID)
        ky, kz = code // GRID, code % GRID
        kx = jnp.where(kx < GRID // 2, kx, kx - GRID)
        direct = ((kz > 0) & (kz < GRID // 2)) | ((kz == 0) & (ky < GRID // 2))
        kx = jnp.where(direct, kx, -kx) + reach
        sign = jnp.where(direct, 1.0, -1.0).astype(jnp.float32)
        hit = (code == first) | (code == second)
        columns = dot(source, jnp.where(hit, 1.0, 0.0).astype(jnp.bfloat16))
        columns = columns.reshape(2, kinds, num_val, tile)
        real = jnp.zeros((num_val, tile), jnp.float32)
        imag = jnp.zeros((num_val, tile), jnp.float32)
        for k in range(kinds):
            keep = jnp.broadcast_to(kx == k, (num_val, tile))
            real = jnp.where(keep, columns[0, k], real)
            imag = jnp.where(keep, columns[1, k], imag)
        out[:, here] = jnp.concatenate([real, imag * sign], axis=0).astype(jnp.bfloat16)
        return carry

    lax.fori_loop(0, out.shape[1] // tile, body, 0)


def transform_pairs(val, cond, gmap, num_waves):
    xs, num_val, plane = val.shape
    waves = gmap.shape[1]
    table, codes, line, reach = tables(num_waves, num_val)
    plane_h, plane_l = np_halves(table)
    line_h, line_l = np_halves(line)
    count = codes.shape[0]
    operands = (val, cond, plane_h, plane_l, line_h, line_l, codes, gmap)
    held = [pltpu.VMEM(x.shape, x.dtype) for x in operands]
    return pl.pallas_call(
        functools.partial(pair_kernel, reach, 256),
        out_shape=jax.ShapeDtypeStruct((2 * num_val, waves), jnp.bfloat16),
        in_specs=[pl.BlockSpec(memory_space=pl.ANY)] * 8,
        out_specs=pl.BlockSpec(memory_space=VMEM),
        scratch_shapes=[
            pltpu.VMEM((xs * num_val, plane), jnp.float32),
            pltpu.VMEM((2 * (2 * reach + 1) * num_val, count), jnp.float32),
        ]
        + held
        + [pltpu.SemaphoreType.DMA((8,))],
        compiler_params=pltpu.CompilerParams(vmem_limit_bytes=62 << 20),
    )(*[jnp.asarray(x) for x in operands])


def expand(held, listed, index, num_val):
    depth, slots = held.shape
    tile = index.shape[1]
    area = GRID * GRID
    lx, ly, lz = listed // area, listed // GRID % GRID, listed % GRID
    mirror = (GRID - lx) % GRID * area + (GRID - ly) % GRID * GRID + (GRID - lz) % GRID
    mirror = jnp.where(listed < 0, -1, mirror)

    def column(row):
        turned = jnp.broadcast_to(row, (128, slots)).T
        return jnp.concatenate([turned] * (tile // 128), axis=1)

    hit = (index == column(listed)) | (index == column(mirror))
    values = dot(held, jnp.where(hit, 1.0, 0.0).astype(jnp.bfloat16))
    kx, ky, kz = index // area, index // GRID % GRID, index % GRID
    low = GRID // 2
    direct = ((kz > 0) & (kz < low)) | (
        (kz == 0) & (((ky > 0) & (ky < low)) | ((ky == 0) & (kx < low)))
    )
    sign = jnp.where(direct, 1.0, -1.0).astype(jnp.float32)
    row = lax.broadcasted_iota(jnp.int32, (depth, tile), 0)
    return values * jnp.where(row // num_val % 2 == 1, sign, 1.0)


def chi_kernel(num_cond, num_val, scalars, gmap, lists, rows, columns, out, scaled):
    num, row_width, tile = out.shape
    depth = rows.shape[0]
    narrow, wide = lists.shape[0], gmap.shape[1] // row_width
    w, n = lax.axis_index("wide"), lax.axis_index("narrow")
    step = pl.program_id(0)

    @pl.when(step == 0)
    def _():
        lane = lax.broadcasted_iota(jnp.int32, (1, depth), 1)
        band, orbital = lane // (2 * num_val), lane % num_val

        def pick(first, count, where):
            def select(i, held):
                return jnp.where(where == i, scalars[first + i], held)

            return lax.fori_loop(0, count, select, jnp.zeros((1, depth), jnp.float32))

        gap = pick(0, num_cond, band) - pick(num_cond, num_val, orbital)
        norm = math.sqrt(num_cond * num_val)
        first = pl.multiple_of(lax.rem(w, wide // narrow) * (row_width // 2), 128)
        listed = lists[w // (wide // narrow), :, pl.ds(first, rows.shape[1])]
        index = gmap[:, pl.ds(pl.multiple_of(w * row_width, 128), row_width)]
        turned = expand(rows[...], listed, index, num_val).T
        for i in range(num):
            omega = scalars[num_cond + num_val + i]
            weight = -2.0 * gap / (gap * gap + omega * omega) / norm
            scaled[i] = (turned * weight).astype(jnp.bfloat16)

    first = pl.multiple_of(step * (tile // 2), 128)
    here = pl.ds(first, window(tile))
    part = gmap.shape[1] // narrow
    index = gmap[:, pl.ds(pl.multiple_of(n * part + step * tile, 128), tile)]
    panel = expand(columns[:, here], lists[n, :, here], index, num_val).astype(jnp.bfloat16)
    for i in range(num):
        out[i] = dot(scaled[i], panel)


def chi_of(eps_cond, eps_val, omega, gmap, lists, rows, columns, row_width, width):
    depth, row_slots = rows.shape
    num = omega.shape[0]
    tile = min(512, width)
    grant = 4 * depth * (row_slots + columns.shape[1]) + 8 * num * row_width * tile
    grant += (2 * num + 16) * row_width * depth + 16 * depth * tile + (8 << 20)
    scalars = jnp.concatenate([eps_cond, eps_val, omega])
    return pl.pallas_call(
        functools.partial(chi_kernel, eps_cond.shape[0], eps_val.shape[0]),
        grid=(width // tile,),
        out_shape=jax.ShapeDtypeStruct((num, row_width, width), jnp.float32),
        in_specs=[
            pl.BlockSpec(memory_space=SMEM),
            pl.BlockSpec(gmap.shape, lambda c: (0, 0)),
            pl.BlockSpec(lists.shape, lambda c: (0, 0, 0)),
            pl.BlockSpec(rows.shape, lambda c: (0, 0)),
            pl.BlockSpec(columns.shape, lambda c: (0, 0)),
        ],
        out_specs=pl.BlockSpec((num, row_width, tile), lambda c: (0, 0, c)),
        scratch_shapes=[pltpu.VMEM((num, row_width, depth), jnp.bfloat16)],
        compiler_params=pltpu.CompilerParams(vmem_limit_bytes=min(grant, 60 << 20)),
    )(scalars, gmap, jnp.asarray(lists), rows, columns)


def body(valence, conduction, eps_val, eps_cond, omega, gmap):
    wide, narrow = lax.axis_size("wide"), lax.axis_size("narrow")
    devices = wide * narrow
    num_val, chunk = valence.shape
    num_local = conduction.shape[0]
    assert num_local == 1
    plane = GRID * GRID
    waves = gmap.shape[0]
    [full] = gather(valence, wide, narrow, 0, 0, 0, 0)
    if chunk != plane:
        full = full.reshape(GRID, devices // GRID, num_val, chunk)
        full = jnp.transpose(full, (0, 2, 1, 3)).reshape(GRID, num_val, plane)
    row_width, width = waves // wide, waves // narrow
    lists = half_lists(waves, narrow, (row_width, min(512, width)))
    wanted = np.maximum(lists.reshape(1, -1), 0)
    local = transform_pairs(full, conduction.reshape(GRID, 1, plane), wanted, waves)
    slots, row_slots = lists.shape[2], window(row_width)
    columns, rows = gather(local, wide, narrow, slots, row_slots, row_width // 2, 1)
    depth = devices * 2 * num_val
    columns, rows = columns.reshape(depth, slots), rows.reshape(depth, row_slots)
    spot = gmap.reshape(1, waves)
    return chi_of(eps_cond, eps_val, omega, spot, lists, rows, columns, row_width, width)


def solution(mesh):
    placed = (P(None, ("wide", "narrow")), P(("wide", "narrow"), None), P(), P(), P(), P())
    return jax.shard_map(
        body, mesh=mesh, in_specs=placed, out_specs=P(None, "wide", "narrow"), check_vma=False
    )
```

```python
import functools
import math

import jax
import jax.numpy as jnp
import numpy as np
from jax import lax
from jax.experimental import pallas as pl
from jax.experimental.pallas import tpu as pltpu
from jax.sharding import PartitionSpec as P

GRID = 32
MESH = pl.DeviceIdType.MESH
VMEM = pltpu.MemorySpace.VMEM
HBM = pltpu.MemorySpace.HBM
SMEM = pltpu.MemorySpace.SMEM


def wide_factors(wide):
    chips = wide // 2
    inner = 2 ** (int(math.log2(chips)) // 2)
    return chips // inner, inner


def gather_kernel(wide, narrow, split, row_width, row_step, src, out, *rest):
    if row_width:
        rows, send_sem, recv_sem, own_sem, row_send, row_recv = rest
    else:
        send_sem, recv_sem, own_sem = rest
    outer, inner = wide_factors(wide)
    w, n = lax.axis_index("wide"), lax.axis_index("narrow")
    core = lax.rem(w, 2)
    y = lax.rem(w // 2, inner)
    z = w // (2 * inner)

    def wide_at(zz, yy, cc):
        return (zz * inner + yy) * 2 + cc

    def slot(zz, yy, cc, nn):
        return wide_at(zz, yy, cc) * narrow + nn

    xs = [lax.rem(n + i, narrow) for i in range(1, narrow)]
    zs = [lax.rem(z + i, outer) for i in range(1, outer)]
    ys = [lax.rem(y + i, inner) for i in range(1, inner)]
    to_x = [(w, nn) for nn in xs]
    to_z = [(wide_at(zz, y, core), n) for zz in zs]
    to_y = [(wide_at(z, yy, core), n) for yy in ys]
    to_core = [(wide_at(z, y, 1 - core), n)]
    peers = to_x + to_z + to_y + to_core

    barrier = pltpu.get_barrier_semaphore()
    for peer in peers:
        pl.semaphore_signal(barrier, inc=1, device_id=peer, device_id_type=MESH)
    pl.semaphore_wait(barrier, len(peers))

    def piece(nn):
        if split:
            return src.at[:, pl.ds(pl.multiple_of(nn * split, split), split)]
        return src

    started = []

    def send(ref, index, target):
        copy = pltpu.make_async_remote_copy(
            src_ref=ref,
            dst_ref=out.at[index],
            send_sem=send_sem.at[len(started)],
            recv_sem=recv_sem.at[index],
            device_id=target,
            device_id_type=MESH,
        )
        copy.start()
        started.append(copy)

    def arrived(index):
        pltpu.make_async_remote_copy(
            src_ref=out.at[index],
            dst_ref=out.at[index],
            send_sem=send_sem.at[0],
            recv_sem=recv_sem.at[index],
            device_id=to_core[0],
            device_id_type=MESH,
        ).wait_recv()

    if row_width:
        holder = w // (wide // narrow)
        first = pl.multiple_of(lax.rem(w, wide // narrow) * row_step, 128)
        group = 2 * narrow

    def row_copy(index, target, start, sem):
        return pltpu.make_async_remote_copy(
            src_ref=out.at[pl.ds(start, group), :, pl.ds(first, row_width)],
            dst_ref=rows.at[pl.ds(start, group)],
            send_sem=row_send.at[sem],
            recv_sem=row_recv.at[index],
            device_id=target,
            device_id_type=MESH,
        )

    chips = [(zz, yy) for yy in [y] + ys for zz in [z] + zs]

    def finish(number):
        zz, yy = chips[number]
        for nn in [n] + xs:
            arrived(slot(zz, yy, 1 - core, nn))
        if row_width:
            @pl.when(n == holder)
            def _():
                for k, target in enumerate(to_x):
                    row_copy(number, target, slot(zz, yy, 0, 0), number * len(to_x) + k).start()

    mine = slot(z, y, core, n)
    for target in to_x:
        send(piece(target[1]), mine, target)
    for target in to_z + to_y + to_core:
        send(piece(n), mine, target)
    own = pltpu.make_async_copy(piece(n), out.at[mine], own_sem)
    own.start()
    for nn in xs:
        index = slot(z, y, core, nn)
        arrived(index)
        for target in to_z + to_y + to_core:
            send(out.at[index], index, target)
    for zz in zs:
        for nn in [n] + xs:
            index = slot(zz, y, core, nn)
            arrived(index)
            for target in to_y + to_core:
                send(out.at[index], index, target)
    own.wait()
    for number in range(outer):
        finish(number)
    for number, (zz, yy) in enumerate(chips[outer:], outer):
        for nn in [n] + xs:
            index = slot(zz, yy, core, nn)
            arrived(index)
            send(out.at[index], index, to_core[0])
        if number > outer:
            finish(number - 1)
    if len(chips) > outer:
        finish(len(chips) - 1)

    for copy in started:
        copy.wait_send()
    if row_width:
        @pl.when(n == holder)
        def _():
            rows[...] = out[:, :, pl.ds(first, row_width)]
            for number, (zz, yy) in enumerate(chips):
                for k, target in enumerate(to_x):
                    row_copy(number, target, slot(zz, yy, 0, 0), number * len(to_x) + k).wait_send()

        @pl.when(n != holder)
        def _():
            for number, (zz, yy) in enumerate(chips):
                row_copy(number, to_x[0], slot(zz, yy, 0, 0), 0).wait_recv()


def gather(src, wide, narrow, split, row_width, row_step, collective_id):
    outer, inner = wide_factors(wide)
    devices = wide * narrow
    n_x, n_z, n_y = narrow - 1, outer - 1, inner - 1
    sends = n_x + n_z + n_y + 1
    sends += n_x * (n_z + n_y + 1) + n_z * narrow * (n_y + 1) + n_y * outer * narrow
    block = (src.shape[0], split or src.shape[1])
    out_shape = [jax.ShapeDtypeStruct((devices,) + block, src.dtype)]
    scratch = [
        pltpu.SemaphoreType.DMA((sends,)),
        pltpu.SemaphoreType.DMA((devices,)),
        pltpu.SemaphoreType.DMA,
    ]
    if row_width:
        out_shape.append(jax.ShapeDtypeStruct((devices, src.shape[0], row_width), src.dtype))
        scratch.append(pltpu.SemaphoreType.DMA((outer * inner * n_x,)))
        scratch.append(pltpu.SemaphoreType.DMA((outer * inner,)))
    return pl.pallas_call(
        functools.partial(gather_kernel, wide, narrow, split, row_width, row_step),
        out_shape=out_shape,
        in_specs=[pl.BlockSpec(memory_space=pl.ANY)],
        out_specs=[pl.BlockSpec(memory_space=VMEM if row_width else pl.ANY)] * len(out_shape),
        scratch_shapes=scratch,
        compiler_params=pltpu.CompilerParams(
            collective_id=collective_id, has_side_effects=True, vmem_limit_bytes=(48 if row_width else 63) << 20
        ),
    )(src)


@functools.lru_cache(None)
def tables(num_waves, num_val):
    fold = np.arange(GRID)
    fold = np.where(fold < GRID // 2, fold, fold - GRID)
    squares = fold**2
    lengths = (squares[:, None, None] + squares[None, :, None] + squares[None, None, :]).reshape(-1)
    limit = int(np.sort(lengths)[num_waves - 1])
    reach = math.isqrt(limit)
    assert reach < GRID // 2
    half = [
        (ky, kz)
        for ky in range(-reach, reach + 1)
        for kz in range(0, reach + 1)
        if ky * ky + kz * kz <= limit and (kz > 0 or ky >= 0)
    ]
    count = -(-len(half) // 128) * 128
    kys = np.array([k for k, _ in half])
    kzs = np.array([k for _, k in half])
    points = np.arange(GRID)
    turn = 2.0 * np.pi / GRID
    phase = (points[:, None, None] * kys + points[None, :, None] * kzs) % GRID
    phase = phase.reshape(GRID * GRID, len(half)) * turn
    plane = np.zeros((GRID * GRID, 2 * count))
    plane[:, : len(half)] = np.cos(phase)
    plane[:, count : count + len(half)] = -np.sin(phase)
    codes = np.full((count, 2), -1, np.int32)
    codes[: len(half), 0] = (kys % GRID) * GRID + kzs % GRID
    codes[: len(half), 1] = (-kys % GRID) * GRID + -kzs % GRID
    kxs = np.arange(-reach, reach + 1)
    line = (kxs[:, None] * points[None, :] % GRID) * turn
    eye = np.eye(num_val)
    norm = 1.0 / math.sqrt(GRID**3)
    cosine = np.kron(np.cos(line), eye) * norm
    sine = np.kron(np.sin(line), eye) * norm
    return plane, codes, np.stack([cosine, sine]), reach


MARGIN = 128


def window(tile):
    return tile // 2 + 2 * MARGIN


@functools.lru_cache(None)
def half_lists(num_waves, narrow, tiles):
    fold = np.arange(GRID)
    fold = np.where(fold < GRID // 2, fold, fold - GRID)
    kx, ky, kz = [k.reshape(-1) for k in np.meshgrid(fold, fold, fold, indexing="ij")]
    lengths = kx * kx + ky * ky + kz * kz
    ordered = np.sort(lengths)[:num_waves]
    half = (kz > 0) | ((kz == 0) & ((ky > 0) | ((ky == 0) & (kx >= 0))))
    chosen = np.nonzero(half & (lengths <= ordered[-1]))[0]
    chosen = chosen[np.argsort(lengths[chosen], kind="stable")]
    sizes = lengths[chosen]
    part = num_waves // narrow
    slots = part // 2 + 2 * MARGIN
    lists = np.full((narrow, 1, slots), -1, np.int32)
    for n in range(narrow):
        begin = np.searchsorted(sizes, ordered[n * part])
        end = np.searchsorted(sizes, ordered[(n + 1) * part - 1], side="right")
        assert end - begin + MARGIN <= slots
        lists[n, 0, MARGIN : MARGIN + end - begin] = chosen[begin:end]
        for tile in tiles:
            for t in range(part // tile):
                g = n * part + t * tile
                low = np.searchsorted(sizes, ordered[g]) - begin + MARGIN
                high = np.searchsorted(sizes, ordered[g + tile - 1], side="right") - begin + MARGIN
                assert t * tile // 2 <= low and high <= t * tile // 2 + window(tile)
    return lists


def np_halves(table):
    table = np.asarray(table, np.float32)
    high = table.astype(jnp.bfloat16)
    return high, (table - high.astype(np.float32)).astype(jnp.bfloat16)


def split_bf16(x):
    high = x.astype(jnp.bfloat16)
    return high, (x - high.astype(jnp.float32)).astype(jnp.bfloat16)


def dot(a, b):
    return jnp.dot(a, b, preferred_element_type=jnp.float32)


def dot3(a, b_high, b_low):
    a_high, a_low = split_bf16(a)
    return dot(a_high, b_high) + (dot(a_low, b_high) + dot(a_high, b_low))


def dot3_left(a_high, a_low, b):
    b_high, b_low = split_bf16(b)
    return dot(a_high, b_high) + (dot(a_high, b_low) + dot(a_low, b_high))


def pair_kernel(reach, tile, *refs):
    sources, out, field, picked = refs[:8], refs[8], refs[9], refs[10]
    held, sems = refs[11:19], refs[19]
    copies = [pltpu.make_async_copy(a, b, sems.at[i]) for i, (a, b) in enumerate(zip(sources, held))]
    for copy in copies:
        copy.start()
    val, cond, plane_h, plane_l, line_h, line_l, codes, gmap = held
    xs, num_val, plane = val.shape
    count = codes.shape[0]
    kinds = 2 * reach + 1
    copies[0].wait()
    copies[1].wait()
    field[...] = (val[...] * cond[...]).reshape(xs * num_val, plane)
    copies[2].wait()
    copies[3].wait()
    step = dot3(field[...], plane_h[...], plane_l[...])
    real, imag = step[:, :count], step[:, count:]
    size = kinds * num_val
    for copy in copies[4:]:
        copy.wait()
    cos_h, sin_h, cos_l, sin_l = line_h[0], line_h[1], line_l[0], line_l[1]
    picked[:size, :] = dot3_left(cos_h, cos_l, real) + dot3_left(sin_h, sin_l, imag)
    picked[size:, :] = dot3_left(cos_h, cos_l, imag) - dot3_left(sin_h, sin_l, real)
    source = picked[...].astype(jnp.bfloat16)
    first, second = codes[:, 0:1], codes[:, 1:2]

    def body(t, carry):
        here = pl.ds(pl.multiple_of(t * tile, tile), tile)
        index = gmap[:, here]
        kx = index // (GRID * GRID)
        code = index % (GRID * GRID)
        ky, kz = code // GRID, code % GRID
        kx = jnp.where(kx < GRID // 2, kx, kx - GRID)
        direct = ((kz > 0) & (kz < GRID // 2)) | ((kz == 0) & (ky < GRID // 2))
        kx = jnp.where(direct, kx, -kx) + reach
        sign = jnp.where(direct, 1.0, -1.0).astype(jnp.float32)
        hit = (code == first) | (code == second)
        columns = dot(source, jnp.where(hit, 1.0, 0.0).astype(jnp.bfloat16))
        columns = columns.reshape(2, kinds, num_val, tile)
        real = jnp.zeros((num_val, tile), jnp.float32)
        imag = jnp.zeros((num_val, tile), jnp.float32)
        for k in range(kinds):
            keep = jnp.broadcast_to(kx == k, (num_val, tile))
            real = jnp.where(keep, columns[0, k], real)
            imag = jnp.where(keep, columns[1, k], imag)
        out[:, here] = jnp.concatenate([real, imag * sign], axis=0).astype(jnp.bfloat16)
        return carry

    lax.fori_loop(0, out.shape[1] // tile, body, 0)


def transform_pairs(val, cond, gmap, num_waves):
    xs, num_val, plane = val.shape
    waves = gmap.shape[1]
    table, codes, line, reach = tables(num_waves, num_val)
    plane_h, plane_l = np_halves(table)
    line_h, line_l = np_halves(line)
    count = codes.shape[0]
    operands = (val, cond, plane_h, plane_l, line_h, line_l, codes, gmap)
    held = [pltpu.VMEM(x.shape, x.dtype) for x in operands]
    return pl.pallas_call(
        functools.partial(pair_kernel, reach, 512 if waves % 512 == 0 else 256),
        out_shape=jax.ShapeDtypeStruct((2 * num_val, waves), jnp.bfloat16),
        in_specs=[pl.BlockSpec(memory_space=pl.ANY)] * 8,
        out_specs=pl.BlockSpec(memory_space=VMEM),
        scratch_shapes=[
            pltpu.VMEM((xs * num_val, plane), jnp.float32),
            pltpu.VMEM((2 * (2 * reach + 1) * num_val, count), jnp.float32),
        ]
        + held
        + [pltpu.SemaphoreType.DMA((8,))],
        compiler_params=pltpu.CompilerParams(vmem_limit_bytes=62 << 20),
    )(*[jnp.asarray(x) for x in operands])


def expand(held, listed, index, num_val):
    depth, slots = held.shape
    tile = index.shape[1]
    area = GRID * GRID
    lx, ly, lz = listed // area, listed // GRID % GRID, listed % GRID
    mirror = (GRID - lx) % GRID * area + (GRID - ly) % GRID * GRID + (GRID - lz) % GRID
    mirror = jnp.where(listed < 0, -1, mirror)

    def column(row):
        turned = jnp.broadcast_to(row, (128, slots)).T
        return jnp.concatenate([turned] * (tile // 128), axis=1)

    hit = (index == column(listed)) | (index == column(mirror))
    values = dot(held, jnp.where(hit, 1.0, 0.0).astype(jnp.bfloat16))
    kx, ky, kz = index // area, index // GRID % GRID, index % GRID
    low = GRID // 2
    direct = ((kz > 0) & (kz < low)) | (
        (kz == 0) & (((ky > 0) & (ky < low)) | ((ky == 0) & (kx < low)))
    )
    sign = jnp.where(direct, 1.0, -1.0).astype(jnp.float32)
    row = lax.broadcasted_iota(jnp.int32, (depth, tile), 0)
    return values * jnp.where(row // num_val % 2 == 1, sign, 1.0)


def chi_kernel(num_cond, num_val, scalars, gmap, lists, rows, columns, out, scaled):
    num, row_width, tile = out.shape
    depth = rows.shape[0]
    narrow, wide = lists.shape[0], gmap.shape[1] // row_width
    w, n = lax.axis_index("wide"), lax.axis_index("narrow")
    step = pl.program_id(0)

    @pl.when(step == 0)
    def _():
        lane = lax.broadcasted_iota(jnp.int32, (1, depth), 1)
        band, orbital = lane // (2 * num_val), lane % num_val

        def pick(first, count, where):
            def select(i, held):
                return jnp.where(where == i, scalars[first + i], held)

            return lax.fori_loop(0, count, select, jnp.zeros((1, depth), jnp.float32))

        gap = pick(0, num_cond, band) - pick(num_cond, num_val, orbital)
        norm = math.sqrt(num_cond * num_val)
        first = pl.multiple_of(lax.rem(w, wide // narrow) * (row_width // 2), 128)
        listed = lists[w // (wide // narrow), :, pl.ds(first, rows.shape[1])]
        index = gmap[:, pl.ds(pl.multiple_of(w * row_width, 128), row_width)]
        turned = expand(rows[...], listed, index, num_val).T
        for i in range(num):
            omega = scalars[num_cond + num_val + i]
            weight = -2.0 * gap / (gap * gap + omega * omega) / norm
            scaled[i] = (turned * weight).astype(jnp.bfloat16)

    first = pl.multiple_of(step * (tile // 2), 128)
    here = pl.ds(first, window(tile))
    part = gmap.shape[1] // narrow
    index = gmap[:, pl.ds(pl.multiple_of(n * part + step * tile, 128), tile)]
    panel = expand(columns[:, here], lists[n, :, here], index, num_val).astype(jnp.bfloat16)
    for i in range(num):
        out[i] = dot(scaled[i], panel)


def chi_of(eps_cond, eps_val, omega, gmap, lists, rows, columns, row_width, width):
    depth, row_slots = rows.shape
    num = omega.shape[0]
    tile = min(512, width)
    grant = 4 * depth * (row_slots + columns.shape[1]) + 8 * num * row_width * tile
    grant += (2 * num + 16) * row_width * depth + 16 * depth * tile + (8 << 20)
    scalars = jnp.concatenate([eps_cond, eps_val, omega])
    return pl.pallas_call(
        functools.partial(chi_kernel, eps_cond.shape[0], eps_val.shape[0]),
        grid=(width // tile,),
        out_shape=jax.ShapeDtypeStruct((num, row_width, width), jnp.float32),
        in_specs=[
            pl.BlockSpec(memory_space=SMEM),
            pl.BlockSpec(gmap.shape, lambda c: (0, 0)),
            pl.BlockSpec(lists.shape, lambda c: (0, 0, 0)),
            pl.BlockSpec(rows.shape, lambda c: (0, 0)),
            pl.BlockSpec(columns.shape, lambda c: (0, 0)),
        ],
        out_specs=pl.BlockSpec((num, row_width, tile), lambda c: (0, 0, c)),
        scratch_shapes=[pltpu.VMEM((num, row_width, depth), jnp.bfloat16)],
        compiler_params=pltpu.CompilerParams(vmem_limit_bytes=min(grant, 60 << 20)),
    )(scalars, gmap, jnp.asarray(lists), rows, columns)


def body(valence, conduction, eps_val, eps_cond, omega, gmap):
    wide, narrow = lax.axis_size("wide"), lax.axis_size("narrow")
    devices = wide * narrow
    num_val, chunk = valence.shape
    num_local = conduction.shape[0]
    assert num_local == 1
    plane = GRID * GRID
    waves = gmap.shape[0]
    [full] = gather(valence, wide, narrow, 0, 0, 0, 0)
    if chunk != plane:
        full = full.reshape(GRID, devices // GRID, num_val, chunk)
        full = jnp.transpose(full, (0, 2, 1, 3)).reshape(GRID, num_val, plane)
    row_width, width = waves // wide, waves // narrow
    lists = half_lists(waves, narrow, (row_width, min(512, width)))
    wanted = np.maximum(lists.reshape(1, -1), 0)
    local = transform_pairs(full, conduction.reshape(GRID, 1, plane), wanted, waves)
    slots, row_slots = lists.shape[2], window(row_width)
    columns, rows = gather(local, wide, narrow, slots, row_slots, row_width // 2, 1)
    depth = devices * 2 * num_val
    columns, rows = columns.reshape(depth, slots), rows.reshape(depth, row_slots)
    spot = gmap.reshape(1, waves)
    return chi_of(eps_cond, eps_val, omega, spot, lists, rows, columns, row_width, width)


def solution(mesh):
    placed = (P(None, ("wide", "narrow")), P(("wide", "narrow"), None), P(), P(), P(), P())
    return jax.shard_map(
        body, mesh=mesh, in_specs=placed, out_specs=P(None, "wide", "narrow"), check_vma=False
    )
```
